32 devices in a mesh: aux: 4 (over y, x), blk: 8 (over z, core).
Axes of the slice: x: 2, y: 2, z: 4, core: 2. Of those that a mesh axis runs over, the one named last changes fastest.
Arguments:
- integrals: bfloat16 [2048, 64, 1024], P(('aux', 'blk')), may hold values from -0.5 to 0.5
- metric: bfloat16 [2048, 512], P('aux'), may hold values from -1 to 2
- pair_list: int32 [15, 2], replicated, may hold values from 0 to 7, as said below
- aux_mask: int32 [16, 8], P('aux'), may hold values 0 or 1
Outputs:
- band_rows: float32 [8, 128, 640], P('blk', 'aux')
The draws below stay inside these ranges and needn't reach their ends.
Inputs may be any that keep to these rules, and one draw needn't show every extreme that they name: `pair_list`: every pair (r, r) appears once; the other rows are distinct pairs (r, r + 1) or (r, r + 2) with both blocks below 8; 7 such rows.
All inputs are finite; a program needn't handle non-finite values. No bound on the sum of `aux_mask` on one device may be relied on, other than what follows from the above.
Results may differ from the reference program's by a relative error of at most 0.0015.
Values may be sent and summed in bfloat16 or wider, within the bound.
A program may use at most 128 MiB of HBM per device.

```python
import math
import jax
import jax.numpy as jnp
from jax import lax

NOCC = 64
QSH = 512
BS = 128
QB = 128
SPAN = 3
NAUX = 2048
NBLK = 8
NQB = 16
N_AUX = 4


def draw_metric(key, part):
    noise_part = jax.random.normal(key, (NAUX, QSH), jnp.float32)
    noise_part = jnp.clip(noise_part, -4.0, 4.0) * (0.5 / math.sqrt(QSH))
    identity = jnp.tile(jnp.eye(QSH, dtype=jnp.float32), (NAUX // QSH, 1))
    return (identity + noise_part).astype(jnp.bfloat16)


def draw_pair_list(key, part):
    first_ids = jnp.arange(NBLK - 1, dtype=jnp.int32)
    second_ids = jnp.arange(NBLK - 2, dtype=jnp.int32)
    rows_off = jnp.concatenate([first_ids, second_ids])
    cols_off = jnp.concatenate([first_ids + 1, second_ids + 2])
    chosen = jax.random.permutation(jax.random.fold_in(key, 11), 2 * NBLK - 3)[:NBLK - 1]
    diagonal = jnp.arange(NBLK, dtype=jnp.int32)
    row_ids = jnp.concatenate([diagonal, rows_off[chosen]])
    col_ids = jnp.concatenate([diagonal, cols_off[chosen]])
    return jnp.stack([row_ids, col_ids], axis=1).astype(jnp.int32)


def plant(drawn, key, low, high):
    longest = drawn.shape.index(max(drawn.shape))
    spots = []
    for shift in (0, 1):
        where = [jax.random.randint(jax.random.fold_in(key, axis), (), 0, length) for axis, length in enumerate(drawn.shape)]
        where[longest] = (where[longest] + shift) % drawn.shape[longest]
        spots.append(tuple(where))
    return drawn.at[spots[0]].set(low).at[spots[1]].set(high)


def steps_of(rng, extent, cuts, low, top_value):
    def one(dim, blocks):
        steps = jax.random.uniform(jax.random.fold_in(jax.random.fold_in(rng, 6), dim), (blocks,), jnp.float32, low / len(cuts), top_value / len(cuts))
        return jnp.repeat(jnp.exp(steps), extent[dim] // blocks).reshape((-1,) + (1,) * (len(extent) - dim - 1))

    loudness = one(*cuts[0])
    for cut in cuts[1:]:
        loudness = loudness * one(*cut)
    return loudness


def normal_values(own_key, extent, spread, bound, cuts=(), kind=jnp.bfloat16):
    array = jax.random.normal(own_key, extent, jnp.float32) * spread
    if len(cuts) > 0:
        array = steps_of(own_key, extent, cuts, -0.22, 0.18) * array
    return jnp.clip(array, min=-bound, max=bound).astype(kind)


def setup_inputs(seed: int = 0) -> dict:
    keys = jax.random.split(jax.random.key(seed), 5)
    integrals = normal_values(keys[0], (NAUX, NOCC, NBLK * BS), 0.07, 0.5, ((0, 32),))
    metric = draw_metric(jax.random.fold_in(keys[4], 71), 0)
    pair_list = draw_pair_list(jax.random.fold_in(keys[4], 71), 0)
    aux_mask = plant((jax.random.randint(keys[3], (NQB, NBLK), 0, 4) < 3).astype(jnp.int32), jax.random.fold_in(keys[3], 1), 0, 1)
    return {"integrals": integrals, "metric": metric, "pair_list": pair_list, "aux_mask": aux_mask}


def fit_all(integrals, metric, aux_mask):
    domains = metric.reshape(N_AUX, QSH, QSH).astype(jnp.float32)
    row_masks = jnp.repeat(aux_mask, QB, axis=0).astype(jnp.float32)

    def fit_one(block_id):
        columns = lax.dynamic_slice_in_dim(integrals, block_id * BS, BS, 2).astype(jnp.float32)
        columns = columns.reshape(N_AUX, QSH, NOCC, BS)
        fitted = jnp.einsum("apq,aqin->apin", domains, columns).reshape(NAUX, NOCC, BS)
        keep_rows = lax.dynamic_slice_in_dim(row_masks, block_id, 1, 1)
        return (fitted * keep_rows[:, :, None]).astype(jnp.bfloat16)

    return lax.map(fit_one, jnp.arange(NBLK, dtype=jnp.int32))


def reference(integrals, metric, pair_list, aux_mask):
    fitted = fit_all(integrals, metric, aux_mask)
    block_ids = jnp.arange(NBLK, dtype=jnp.int32)
    offsets = jnp.arange(SPAN, dtype=jnp.int32)
    col_gap = pair_list[:, 1] - pair_list[:, 0]
    hits = (pair_list[:, 0][:, None, None] == block_ids[None, :, None]) & (col_gap[:, None, None] == offsets[None, None, :])
    listed = jnp.sum(hits.astype(jnp.int32), axis=0).astype(jnp.float32)

    def row_tiles(block_id):
        own_block = fitted[block_id].reshape(-1, BS).astype(jnp.float32)
        tile_list = []
        for distance in range(SPAN):
            partner_id = jnp.minimum(block_id + distance, NBLK - 1)
            partner = fitted[partner_id].reshape(-1, BS).astype(jnp.float32)
            tile_list.append(lax.dot_general(own_block, partner, (((0,), (0,)), ((), ())), preferred_element_type=jnp.float32))
        return jnp.stack(tile_list)

    upper_tiles = lax.map(row_tiles, block_ids) * listed[:, :, None, None]
    pieces = []
    for column_slot in range(2 * SPAN - 1):
        offset = column_slot - (SPAN - 1)
        if offset >= 0:
            pieces.append(upper_tiles[:, offset])
        else:
            distance = -offset
            shifted = jnp.concatenate([jnp.zeros((distance, BS, BS), jnp.float32), upper_tiles[: NBLK - distance, distance]], axis=0)
            pieces.append(jnp.swapaxes(shifted, 1, 2))
    return jnp.concatenate(pieces, axis=2)
```

```python
import functools

import jax
import jax.numpy as jnp
from jax import lax
from jax.experimental import pallas as pl
from jax.experimental.pallas import tpu as pltpu
from jax.sharding import PartitionSpec as P

BS = 128
QB = 128
SPAN = 3
SUB = 8
PAIR = 2
MESH = pl.DeviceIdType.MESH


def tile_kernel(
    peers, domains, blocks, depth, mask_hbm, pairs_hbm, metric_hbm, x_ref, out_ref,
    mask_ref, pairs_ref, metric_ref,
    slab, wide, ordered, fit_rows, fit_cols, piece_out, piece_in, sum_out, sum_in, relay_in,
    tail_out, tail_in, weights,
    send_sem, recv_sem, own_sem, piece_send, piece_recv, sum_send, sum_recv, relay_send,
    relay_recv, tail_send, tail_recv, load_sem,
):
    me = lax.axis_index("blk")
    domain = lax.axis_index("aux")
    rows = depth // peers
    half = peers // 2
    last = blocks - 1
    group = domains * PAIR
    strip = BS // group
    pair_base = (me // PAIR) * PAIR
    place = domain * PAIR + lax.rem(me, PAIR)
    slots = 2 * SPAN - 1
    side = me // half

    def mirror(index, which):
        return index + which * (peers - 1 - 2 * index)

    rank = mirror(me, side)
    outer = rank < PAIR
    is_tail = rank == 0
    sign = 2 * side - 1

    def block_at(step, which):
        return mirror(step, 1 - which)

    loads = [
        pltpu.make_async_copy(mask_hbm, mask_ref, load_sem.at[0]),
        pltpu.make_async_copy(pairs_hbm, pairs_ref, load_sem.at[1]),
        pltpu.make_async_copy(metric_hbm, metric_ref, load_sem.at[2]),
    ]
    for load in loads:
        load.start()
    barrier = pltpu.get_barrier_semaphore()

    def member(off):
        other = lax.rem(place + off, group)
        return {"aux": other // PAIR, "blk": pair_base + lax.rem(other, PAIR)}

    def greet(off, carry):
        pl.semaphore_signal(
            barrier, inc=1, device_id={"blk": lax.rem(me + off, peers)}, device_id_type=MESH
        )
        return carry

    lax.fori_loop(1, peers, greet, 0)
    for turn in range(1, domains):
        for near in range(half):
            pl.semaphore_signal(
                barrier,
                inc=1,
                device_id={"aux": lax.rem(domain + turn, domains), "blk": side * half + near},
                device_id_type=MESH,
            )
    pl.semaphore_wait(barrier, peers - 1 + (domains - 1) * half)

    def source(block, target):
        return x_ref.at[
            :,
            pl.ds(pl.multiple_of(target * SUB, SUB), SUB),
            pl.ds(pl.multiple_of(block * BS, BS), BS),
        ]

    def landing(step, sender):
        return slab.at[step, pl.ds(pl.multiple_of(sender * rows, rows), rows)]

    def outgoing(step, target):
        return pltpu.make_async_remote_copy(
            src_ref=source(block_at(step, target // half), target),
            dst_ref=landing(step, me),
            send_sem=send_sem.at[step, target],
            recv_sem=recv_sem.at[step, me],
            device_id={"blk": target},
            device_id_type=MESH,
        )

    def incoming(step, sender):
        return pltpu.make_async_remote_copy(
            src_ref=source(block_at(step, side), me),
            dst_ref=landing(step, sender),
            send_sem=send_sem.at[step, sender],
            recv_sem=recv_sem.at[step, sender],
            device_id={"blk": sender},
            device_id_type=MESH,
        )

    def own(step):
        return pltpu.make_async_copy(
            source(block_at(step, side), me), landing(step, me), own_sem.at[step]
        )

    def beside(off):
        return side * half + lax.rem(me + off, half)

    def across(other_rank):
        return mirror(other_rank, 1 - side)

    def launch(step, carry):
        for other_rank in range(half - 1, 0, -1):
            outgoing(step, across(other_rank)).start()

        @pl.when(step < last - 1)
        def _():
            outgoing(step, across(0)).start()

        for off in range(1, half):
            outgoing(step, beside(off)).start()
        own(step).start()
        return carry

    lax.fori_loop(0, blocks, launch, 0)
    for step in (last - 1, last):
        outgoing(step, across(0)).start()

    for load in loads:
        load.wait()
    for slot in range(slots):
        gap = abs(slot - (SPAN - 1))
        behind = jnp.minimum(sign * (slot - (SPAN - 1)), 0)
        count = jnp.int32(0)
        for index in range(pairs_ref.shape[1]):
            first = pairs_ref[0, index]
            hit = (first == me + behind) & (pairs_ref[1, index] - first == gap)
            count = count + hit.astype(jnp.int32)
        weights[slot] = count.astype(jnp.float32)

    fit_cols[: (SPAN - 1) * BS, :] = jnp.zeros(((SPAN - 1) * BS, SUB * depth), jnp.bfloat16)
    for gap in range(1, SPAN):

        @pl.when(rank < gap)
        def _():
            sum_in[pl.ds(side * half, half), SPAN - 1 + gap] = jnp.zeros(
                (half, strip, BS), jnp.float32
            )

    def piece_to(step, off):
        return pltpu.make_async_remote_copy(
            src_ref=piece_out.at[step, lax.rem(place + off, group)],
            dst_ref=piece_in.at[step, place],
            send_sem=piece_send.at[step, off],
            recv_sem=piece_recv.at[step, off],
            device_id=member(off),
            device_id_type=MESH,
        )

    def piece_from(step, off):
        sender = lax.rem(place - off + group, group)
        return pltpu.make_async_remote_copy(
            src_ref=piece_out.at[step, sender],
            dst_ref=piece_in.at[step, sender],
            send_sem=piece_send.at[step, off],
            recv_sem=piece_recv.at[step, off],
            device_id=member(group - off),
            device_id_type=MESH,
        )

    def span_of(gap):
        return pl.ds(0, SPAN) if gap == 0 else pl.ds(SPAN - 1 + gap, 1)

    def sum_to(step, gap):
        return pltpu.make_async_remote_copy(
            src_ref=sum_out.at[step, span_of(gap)],
            dst_ref=sum_in.at[me, span_of(gap)],
            send_sem=sum_send.at[step, gap],
            recv_sem=sum_recv.at[me, gap],
            device_id={"blk": block_at(step - gap, side)},
            device_id_type=MESH,
        )

    def sum_from(sender, gap):
        return pltpu.make_async_remote_copy(
            src_ref=sum_out.at[0, span_of(gap)],
            dst_ref=sum_in.at[sender, span_of(gap)],
            send_sem=sum_send.at[0, gap],
            recv_sem=sum_recv.at[sender, gap],
            device_id={"blk": sender},
            device_id_type=MESH,
        )

    def relay(step, gap, other_rank):
        return pltpu.make_async_remote_copy(
            src_ref=sum_out.at[step, span_of(gap)],
            dst_ref=relay_in.at[step, span_of(gap)],
            send_sem=relay_send.at[step, gap],
            recv_sem=relay_recv.at[step, gap],
            device_id={"blk": mirror(other_rank, side)},
            device_id_type=MESH,
        )

    def crossing(step, gap):
        return (step >= gap) & (step - gap < half)

    def staying(step, gap):
        return step - gap >= half

    def gather(step):
        late = outer & (step >= last - 1)

        def arrive(off, inner):
            sender = lax.rem(place - off + group, group)

            @pl.when(jnp.logical_not(late & (lax.rem(sender, PAIR) == side)))
            def _():
                piece_from(step, off).wait_recv()

            return inner

        lax.fori_loop(1, group, arrive, 0)

        @pl.when(late)
        def _():
            total = piece_in[step, 1 - side]
            for turn in range(1, domains):
                total = total + piece_in[step, turn * PAIR + 1 - side]
            sum_out[step] = total

        @pl.when(jnp.logical_not(late))
        def _():
            total = piece_in[step, 0]
            for other in range(1, group):
                total = total + piece_in[step, other]
            sum_out[step] = total

        for gap in range(SPAN):
            owner = block_at(step - gap, side)

            @pl.when(staying(step, gap) & (owner == me))
            def _():
                if gap == 0:
                    sum_in[me, :SPAN] = sum_out[step, :SPAN]
                else:
                    sum_in[me, SPAN - 1 + gap] = sum_out[step, SPAN - 1 + gap]

            @pl.when(staying(step, gap) & (owner != me))
            def _():
                sum_to(step, gap).start()

            @pl.when(crossing(step, gap) & outer)
            def _():
                relay(step, gap, rank + PAIR).start()

    def forward(step):
        for gap in range(SPAN):

            @pl.when(crossing(step, gap) & jnp.logical_not(outer))
            def _():
                relay(step, gap, rank - PAIR).wait_recv()
                if gap == 0:
                    sum_out[step, :SPAN] = sum_out[step, :SPAN] + relay_in[step, :SPAN]
                else:
                    at = SPAN - 1 + gap
                    sum_out[step, at] = sum_out[step, at] + relay_in[step, at]
                sum_to(step, gap).start()

    def reorder(step, sender):
        span = pl.ds(pl.multiple_of(sender * rows, rows), rows)
        wide[...] = slab[step, span].reshape(rows * SUB, BS).astype(jnp.float32)
        for i in range(SUB):
            ordered[span, i * BS : (i + 1) * BS] = wide[pl.ds(i, rows, stride=SUB), :].astype(
                jnp.bfloat16
            )

    def collect(step):
        own(step).wait()
        reorder(step, me)

        def arrive_beside(off, inner):
            incoming(step, beside(off)).wait_recv()
            reorder(step, beside(off))
            return inner

        def arrive_across(other_rank, inner):
            incoming(step, across(other_rank)).wait_recv()
            reorder(step, across(other_rank))
            return inner

        lax.fori_loop(1, half, arrive_beside, 0)
        lax.fori_loop(0, half, arrive_across, 0)

    def multiply(step):
        block = block_at(step, side)
        for qb in range(depth // QB):
            keep = mask_ref[qb, block].astype(jnp.float32)
            fitted = jnp.dot(
                metric_ref[qb * QB : (qb + 1) * QB, :],
                ordered[...],
                preferred_element_type=jnp.float32,
            )
            fitted = (fitted * keep).astype(jnp.bfloat16)
            for i in range(SUB):
                piece = fitted[:, i * BS : (i + 1) * BS]
                at = i * depth + qb * QB
                fit_rows[at : at + QB, :] = piece
                fit_cols[
                    pl.ds(pl.multiple_of((step + SPAN - 1) * BS, BS), BS), at : at + QB
                ] = piece.T
        return jnp.dot(
            fit_cols[pl.ds(pl.multiple_of(step * BS, BS), SPAN * BS), :],
            fit_rows[...],
            preferred_element_type=jnp.float32,
        )

    def pieces(step, tiles):
        for gap in range(SPAN):
            at = (SPAN - 1 - gap) * BS
            tile = tiles[at : at + BS, :]
            piece_out[step, :, SPAN - 1 + gap] = tile.reshape(group, strip, BS)
            if gap > 0:
                piece_out[step, :, SPAN - 1 - gap] = tile.T.reshape(group, strip, BS)
        piece_in[step, place] = piece_out[step, place]

        def one(off, inner):
            piece_to(step, off).start()
            return inner

        lax.fori_loop(1, group, one, 0)

    def tail_to(turn_step, gap, turn):
        to = lax.rem(domain + turn, domains)
        return pltpu.make_async_remote_copy(
            src_ref=tail_out.at[turn_step, to, span_of(gap)],
            dst_ref=tail_in.at[turn_step, domain, span_of(gap)],
            send_sem=tail_send.at[turn_step, gap, turn],
            recv_sem=tail_recv.at[turn_step, gap, domain],
            device_id={"aux": to, "blk": mirror(1 - turn_step + gap, side)},
            device_id_type=MESH,
        )

    def tail_from(turn_step, gap, sender):
        return pltpu.make_async_remote_copy(
            src_ref=tail_out.at[turn_step, sender, span_of(gap)],
            dst_ref=tail_in.at[turn_step, sender, span_of(gap)],
            send_sem=tail_send.at[turn_step, gap, 0],
            recv_sem=tail_recv.at[turn_step, gap, sender],
            device_id={"aux": sender, "blk": mirror(0, side)},
            device_id_type=MESH,
        )

    def tail_sends():
        for turn_step in range(2):
            for gap in range(SPAN):
                for turn in range(domains):
                    if turn > 0 or turn_step == 0 or gap > 0:
                        yield turn_step, gap, turn

    def direct(turn_step, tiles):
        for gap in range(SPAN):
            at = (SPAN - 1 - gap) * BS
            tile = tiles[at : at + BS, :]
            low = (domains, BS // domains, BS)
            tail_out[turn_step, :, SPAN - 1 + gap] = tile.reshape(low).astype(jnp.bfloat16)
            if gap > 0:
                tail_out[turn_step, :, SPAN - 1 - gap] = tile.T.reshape(low).astype(jnp.bfloat16)
        for which, gap, turn in tail_sends():
            if which == turn_step:
                tail_to(turn_step, gap, turn).start()
        if turn_step == 1:
            tail_in[1, domain, :SPAN] = tail_out[1, domain, :SPAN]

    def step(index, carry):
        @pl.when(index > 0)
        def _():
            gather(index - 1)

        @pl.when(index > 1)
        def _():
            forward(index - 2)

        @pl.when(is_tail & (index == last))
        def _():
            gather(last)

        collect(index)
        tiles = multiply(index)
        late = is_tail & (index >= last - 1)

        @pl.when(jnp.logical_not(late))
        def _():
            pieces(index, tiles)

        for turn_step in range(2):

            @pl.when(is_tail & (index == last - 1 + turn_step))
            def _():
                direct(turn_step, tiles)

        return carry

    lax.fori_loop(0, blocks, step, 0)

    @pl.when(jnp.logical_not(is_tail))
    def _():
        gather(last)

    def settle(index, carry):
        for other_rank in range(half):
            outgoing(index, across(other_rank)).wait_send()
        for off in range(1, half):
            outgoing(index, beside(off)).wait_send()

        def two(off, inner):
            piece_to(index, off).wait_send()
            return inner

        @pl.when(jnp.logical_not(is_tail & (index >= last - 1)))
        def _():
            lax.fori_loop(1, group, two, 0)

        for gap in range(SPAN):
            owner = block_at(index - gap, side)
            kept = staying(index, gap) & (owner != me)
            crossed = crossing(index, gap)

            @pl.when(kept | (crossed & jnp.logical_not(outer)))
            def _():
                sum_to(index, gap).wait_send()

            @pl.when(crossed & outer)
            def _():
                relay(index, gap, rank + PAIR).wait_send()

        return carry

    lax.fori_loop(0, blocks, settle, 0)

    inner_base = half - PAIR + (1 - side) * PAIR
    for gap in range(SPAN):

        @pl.when(rank >= gap)
        def _():
            def arrive(off, inner):
                sum_from(beside(off), gap).wait_recv()
                return inner

            lax.fori_loop(1, half, arrive, 0)

        for core in range(PAIR):
            sum_from(inner_base + core, gap).wait_recv()

    for turn_step in range(2):
        for gap in range(SPAN):

            @pl.when(rank == 1 - turn_step + gap)
            def _():
                for sender in range(domains):

                    @pl.when(jnp.logical_not(is_tail & (sender == domain)))
                    def _():
                        tail_from(turn_step, gap, sender).wait_recv()

    for slot in range(slots):
        where = SPAN - 1 + sign * (slot - (SPAN - 1))
        columns = pl.ds(pl.multiple_of(where * BS, BS), BS)
        for core in range(PAIR):
            total = sum_in[inner_base + core, slots - 1 - slot]
            for turn in range(half // PAIR):
                total = total + sum_in[side * half + turn * PAIR + core, slot]
            out_ref[0, core * strip : (core + 1) * strip, columns] = total * weights[slot]

    for turn_step in range(2):
        for gap in range(SPAN):

            @pl.when(rank == 1 - turn_step + gap)
            def _():
                for slot in range(SPAN) if gap == 0 else [SPAN - 1 + gap]:
                    where = SPAN - 1 + sign * (slot - (SPAN - 1))
                    columns = pl.ds(pl.multiple_of(where * BS, BS), BS)
                    total = tail_in[turn_step, 0, slot].astype(jnp.float32)
                    for sender in range(1, domains):
                        total = total + tail_in[turn_step, sender, slot].astype(jnp.float32)
                    out_ref[0, :, columns] = out_ref[0, :, columns] + total * weights[slot]

    for which, gap, turn in tail_sends():

        @pl.when(is_tail)
        def _():
            tail_to(which, gap, turn).wait_send()


def in_hbm(operand):
    return pltpu.with_memory_space_constraint(operand, pltpu.MemorySpace.HBM)


def by_orbital(integrals, metric, pair_list, aux_mask):
    peers = lax.axis_size("blk")
    domains = lax.axis_size("aux")
    depth = metric.shape[1]
    blocks = aux_mask.shape[1]
    group = domains * PAIR
    slots = 2 * SPAN - 1
    strip = BS // group
    return pl.pallas_call(
        functools.partial(tile_kernel, peers, domains, blocks, depth),
        out_shape=jax.ShapeDtypeStruct((1, BS // domains, slots * BS), jnp.float32),
        in_specs=[
            pl.BlockSpec(memory_space=pl.ANY),
            pl.BlockSpec(memory_space=pl.ANY),
            pl.BlockSpec(memory_space=pl.ANY),
            pl.BlockSpec(memory_space=pl.ANY),
        ],
        out_specs=pl.BlockSpec(memory_space=pltpu.VMEM),
        scratch_shapes=[
            pltpu.SMEM(aux_mask.shape, jnp.int32),
            pltpu.SMEM(pair_list.shape[::-1], jnp.int32),
            pltpu.VMEM(metric.shape, jnp.bfloat16),
            pltpu.VMEM((blocks, depth, SUB, BS), jnp.bfloat16),
            pltpu.VMEM((depth // peers * SUB, BS), jnp.float32),
            pltpu.VMEM((depth, SUB * BS), jnp.bfloat16),
            pltpu.VMEM((SUB * depth, BS), jnp.bfloat16),
            pltpu.VMEM(((blocks + SPAN - 1) * BS, SUB * depth), jnp.bfloat16),
            pltpu.VMEM((blocks, group, slots, strip, BS), jnp.float32),
            pltpu.VMEM((blocks, group, slots, strip, BS), jnp.float32),
            pltpu.VMEM((blocks, slots, strip, BS), jnp.float32),
            pltpu.VMEM((peers, slots, strip, BS), jnp.float32),
            pltpu.VMEM((blocks, slots, strip, BS), jnp.float32),
            pltpu.VMEM((2, domains, slots, BS // domains, BS), jnp.bfloat16),
            pltpu.VMEM((2, domains, slots, BS // domains, BS), jnp.bfloat16),
            pltpu.SMEM((slots,), jnp.float32),
            pltpu.SemaphoreType.DMA((blocks, peers)),
            pltpu.SemaphoreType.DMA((blocks, peers)),
            pltpu.SemaphoreType.DMA((blocks,)),
            pltpu.SemaphoreType.DMA((blocks, group)),
            pltpu.SemaphoreType.DMA((blocks, group)),
            pltpu.SemaphoreType.DMA((blocks, SPAN)),
            pltpu.SemaphoreType.DMA((peers, SPAN)),
            pltpu.SemaphoreType.DMA((blocks, SPAN)),
            pltpu.SemaphoreType.DMA((blocks, SPAN)),
            pltpu.SemaphoreType.DMA((2, SPAN, domains)),
            pltpu.SemaphoreType.DMA((2, SPAN, domains)),
            pltpu.SemaphoreType.DMA((3,)),
        ],
        compiler_params=pltpu.CompilerParams(
            collective_id=0, has_side_effects=True, vmem_limit_bytes=36 * 1024 * 1024
        ),
    )(*[in_hbm(operand) for operand in (aux_mask, pair_list.T, metric, integrals)])


def from_behind(array, axis, by):
    peers = lax.axis_size(axis)
    pairs = [(i, i + by) for i in range(peers) if 0 <= i + by < peers]
    return lax.ppermute(array, axis, pairs)


def fit_block(metric, slab_piece, mask_rows):
    fitted = jnp.einsum("pq,qjn->pjn", metric, slab_piece, preferred_element_type=jnp.float32)
    return (fitted * mask_rows[:, None, None]).astype(jnp.bfloat16)


def by_block(integrals, metric, pair_list, aux_mask):
    block_count = aux_mask.shape[1]
    position = lax.axis_index("blk")
    block_ids = jnp.arange(block_count, dtype=jnp.int32)
    offsets = jnp.arange(SPAN, dtype=jnp.int32)
    col_gap = pair_list[:, 1] - pair_list[:, 0]
    hits = (pair_list[:, 0][:, None] == position) & (col_gap[:, None] == offsets[None, :])
    listed = jnp.sum(hits.astype(jnp.int32), axis=0)
    one_hot = (block_ids == position).astype(jnp.int32)
    column = jnp.sum(aux_mask * one_hot[None, :], axis=1)
    own_mask = jnp.repeat(column, QB).astype(jnp.float32)
    own_block = fit_block(
        metric, lax.all_to_all(integrals, "blk", split_axis=2, concat_axis=0, tiled=True), own_mask
    )
    partners = [own_block]
    current = own_block
    for turn_index in range(SPAN - 1):
        current = from_behind(current, "blk", -1)
        partners.append(current)
    flat_own = partners[0].reshape(-1, BS)

    def make_tile(partner):
        return lax.dot_general(
            flat_own,
            partner.reshape(-1, BS),
            (((0,), (0,)), ((), ())),
            preferred_element_type=jnp.float32,
        )

    tile_list = [
        make_tile(partners[offset]) * listed[offset].astype(jnp.float32) for offset in range(SPAN)
    ]
    upper_tiles = jnp.stack(tile_list)
    mirror_tiles = jnp.stack([jnp.transpose(tile_list[offset]) for offset in range(1, SPAN)])
    lower_tiles = []
    moving = mirror_tiles
    for turn_index in range(SPAN - 1):
        moving = from_behind(moving.astype(jnp.bfloat16), "blk", 1).astype(moving.dtype)
        lower_tiles.append(moving[0])
        moving = moving[1:]
    whole_band = jnp.concatenate(
        [jnp.stack([lower_tiles[SPAN - 2 - slot] for slot in range(SPAN - 1)]), upper_tiles], axis=0
    )
    band_parts = lax.psum_scatter(whole_band, "aux", scatter_dimension=1, tiled=True)
    pieces = [band_parts[slot] for slot in range(2 * SPAN - 1)]
    band_rows = jnp.concatenate(pieces, axis=1)
    return band_rows[None]


def local(integrals, metric, pair_list, aux_mask):
    peers = lax.axis_size("blk")
    blocks = aux_mask.shape[1]
    strips = BS % (8 * PAIR * lax.axis_size("aux")) == 0 and peers == 4 * PAIR
    whole_tiles = integrals.shape[1] == SUB * peers and blocks == peers and strips
    if whole_tiles:
        return by_orbital(integrals, metric, pair_list, aux_mask)
    return by_block(integrals, metric, pair_list, aux_mask)


def solution(mesh):
    return jax.shard_map(
        local,
        mesh=mesh,
        in_specs=(P(("aux", "blk"), None, None), P("aux", None), P(), P("aux", None)),
        out_specs=P("blk", "aux", None),
        check_vma=False,
    )
```

```python
import functools

import jax
import jax.numpy as jnp
from jax import lax
from jax.experimental import pallas as pl
from jax.experimental.pallas import tpu as pltpu
from jax.sharding import PartitionSpec as P

BS = 128
QB = 128
SPAN = 3
SUB = 8
PAIR = 2
MESH = pl.DeviceIdType.MESH


def tile_kernel(
    peers, domains, blocks, depth, mask_hbm, pairs_hbm, metric_hbm, x_ref, out_ref,
    mask_ref, pairs_ref, metric_ref,
    slab, wide, ordered, fit_rows, fit_cols, piece_out, piece_in, sum_out, sum_in,
    tail_out, tail_in, weights,
    send_sem, recv_sem, piece_send, piece_recv, sum_send, sum_recv, cross_send,
    tail_send, tail_recv, load_sem,
):
    me = lax.axis_index("blk")
    domain = lax.axis_index("aux")
    rows = depth // peers
    half = peers // 2
    last = blocks - 1
    group = domains * PAIR
    strip = BS // group
    pair_base = (me // PAIR) * PAIR
    place = domain * PAIR + lax.rem(me, PAIR)
    slots = 2 * SPAN - 1
    side = me // half

    def mirror(index, which):
        return index + which * (peers - 1 - 2 * index)

    rank = mirror(me, side)
    outer = rank < PAIR
    is_tail = rank == 0
    sign = 2 * side - 1

    def block_at(step, which):
        return mirror(step, 1 - which)

    loads = [
        pltpu.make_async_copy(mask_hbm, mask_ref, load_sem.at[0]),
        pltpu.make_async_copy(pairs_hbm, pairs_ref, load_sem.at[1]),
        pltpu.make_async_copy(metric_hbm, metric_ref, load_sem.at[2]),
    ]
    for load in loads:
        load.start()
    barrier = pltpu.get_barrier_semaphore()

    def member(off):
        other = lax.rem(place + off, group)
        return {"aux": other // PAIR, "blk": pair_base + lax.rem(other, PAIR)}

    def greet(off, carry):
        pl.semaphore_signal(
            barrier, inc=1, device_id={"blk": lax.rem(me + off, peers)}, device_id_type=MESH
        )
        return carry

    lax.fori_loop(1, peers, greet, 0)
    for turn in range(1, domains):
        for near in range(half):
            pl.semaphore_signal(
                barrier,
                inc=1,
                device_id={"aux": lax.rem(domain + turn, domains), "blk": side * half + near},
                device_id_type=MESH,
            )
    pl.semaphore_wait(barrier, peers - 1 + (domains - 1) * half)

    def source(block, target):
        return x_ref.at[
            :,
            pl.ds(pl.multiple_of(target * SUB, SUB), SUB),
            pl.ds(pl.multiple_of(block * BS, BS), BS),
        ]

    def landing(step, sender):
        return slab.at[step, pl.ds(pl.multiple_of(sender * rows, rows), rows)]

    def outgoing(step, target):
        return pltpu.make_async_remote_copy(
            src_ref=source(block_at(step, target // half), target),
            dst_ref=landing(step, me),
            send_sem=send_sem.at[step],
            recv_sem=recv_sem.at[step],
            device_id={"blk": target},
            device_id_type=MESH,
        )

    def settled(ref, sem):
        pltpu.make_async_copy(ref, ref, sem).wait()

    def own(step):
        return pltpu.make_async_copy(
            source(block_at(step, side), me), landing(step, me), recv_sem.at[step]
        )

    def beside(off):
        return side * half + lax.rem(me + off, half)

    def across(other_rank):
        return mirror(other_rank, 1 - side)

    def launch(step, carry):
        for other_rank in range(half - 1, 0, -1):
            outgoing(step, across(other_rank)).start()

        @pl.when(step < last - 1)
        def _():
            outgoing(step, across(0)).start()

        for off in range(1, half):
            outgoing(step, beside(off)).start()
        own(step).start()
        return carry

    lax.fori_loop(0, blocks, launch, 0)
    for step in (last - 1, last):
        outgoing(step, across(0)).start()

    for load in loads:
        load.wait()
    for slot in range(slots):
        gap = abs(slot - (SPAN - 1))
        behind = jnp.minimum(sign * (slot - (SPAN - 1)), 0)
        count = jnp.int32(0)
        for index in range(pairs_ref.shape[1]):
            first = pairs_ref[0, index]
            hit = (first == me + behind) & (pairs_ref[1, index] - first == gap)
            count = count + hit.astype(jnp.int32)
        weights[slot] = count.astype(jnp.float32)

    fit_cols[: (SPAN - 1) * BS, :] = jnp.zeros(((SPAN - 1) * BS, SUB * depth), jnp.bfloat16)
    for gap in range(1, SPAN):

        @pl.when(rank < gap)
        def _():
            sum_in[pl.ds(side * half, half), SPAN - 1 + gap] = jnp.zeros(
                (half, strip, BS), jnp.float32
            )

    def piece_to(step, off):
        return pltpu.make_async_remote_copy(
            src_ref=piece_out.at[step, lax.rem(place + off, group)],
            dst_ref=piece_in.at[step, place],
            send_sem=piece_send.at[step],
            recv_sem=piece_recv.at[step],
            device_id=member(off),
            device_id_type=MESH,
        )

    def span_of(gap):
        return pl.ds(0, SPAN) if gap == 0 else pl.ds(SPAN - 1 + gap, 1)

    def sum_to(step, gap, sem):
        return pltpu.make_async_remote_copy(
            src_ref=sum_out.at[step, span_of(gap)],
            dst_ref=sum_in.at[me, span_of(gap)],
            send_sem=sem,
            recv_sem=sum_recv.at[gap],
            device_id={"blk": block_at(step - gap, side)},
            device_id_type=MESH,
        )

    def crossing(step, gap):
        return (step >= gap) & (step - gap < half)

    def staying(step, gap):
        return step - gap >= half

    def shipped(step, gap):
        return staying(step, gap) & (block_at(step - gap, side) != me)

    def ship():
        def one(step, inner):
            for gap in range(SPAN):

                @pl.when(crossing(step, gap))
                def _():
                    sum_to(step, gap, cross_send.at[0]).start()

            return inner

        lax.fori_loop(0, half + SPAN - 1, one, 0)

    def gather(step):
        late = outer & (step >= last - 1)

        @pl.when(late & is_tail)
        def _():
            settled(piece_in.at[step, pl.ds(0, domains)], piece_recv.at[step])

        @pl.when(late & jnp.logical_not(is_tail))
        def _():
            settled(piece_in.at[step, pl.ds(0, domains - 1)], piece_recv.at[step])

        @pl.when(jnp.logical_not(late))
        def _():
            settled(piece_in.at[step, pl.ds(0, group - 1)], piece_recv.at[step])

        @pl.when(late)
        def _():
            total = piece_in[step, 1 - side]
            for turn in range(1, domains):
                total = total + piece_in[step, turn * PAIR + 1 - side]
            sum_out[step] = total

        @pl.when(jnp.logical_not(late))
        def _():
            total = piece_in[step, 0]
            for other in range(1, group):
                total = total + piece_in[step, other]
            sum_out[step] = total

        for gap in range(SPAN):
            owner = block_at(step - gap, side)

            @pl.when(staying(step, gap) & (owner == me))
            def _():
                if gap == 0:
                    sum_in[me, :SPAN] = sum_out[step, :SPAN]
                else:
                    sum_in[me, SPAN - 1 + gap] = sum_out[step, SPAN - 1 + gap]

            @pl.when(shipped(step, gap))
            def _():
                sum_to(step, gap, sum_send.at[gap]).start()

    def reorder(step, sender):
        span = pl.ds(pl.multiple_of(sender * rows, rows), rows)
        wide[...] = slab[step, span].reshape(rows * SUB, BS).astype(jnp.float32)
        for i in range(SUB):
            ordered[span, i * BS : (i + 1) * BS] = wide[pl.ds(i, rows, stride=SUB), :].astype(
                jnp.bfloat16
            )

    def collect(step):
        settled(slab.at[step], recv_sem.at[step])

        def one(sender, inner):
            reorder(step, sender)
            return inner

        lax.fori_loop(0, peers, one, 0)

    def multiply(step):
        block = block_at(step, side)
        for qb in range(depth // QB):
            keep = mask_ref[qb, block].astype(jnp.float32)
            fitted = jnp.dot(
                metric_ref[qb * QB : (qb + 1) * QB, :],
                ordered[...],
                preferred_element_type=jnp.float32,
            )
            fitted = (fitted * keep).astype(jnp.bfloat16)
            for i in range(SUB):
                piece = fitted[:, i * BS : (i + 1) * BS]
                at = i * depth + qb * QB
                fit_rows[at : at + QB, :] = piece
                fit_cols[
                    pl.ds(pl.multiple_of((step + SPAN - 1) * BS, BS), BS), at : at + QB
                ] = piece.T
        return jnp.dot(
            fit_cols[pl.ds(pl.multiple_of(step * BS, BS), SPAN * BS), :],
            fit_rows[...],
            preferred_element_type=jnp.float32,
        )

    def pieces(step, tiles):
        for gap in range(SPAN):
            at = (SPAN - 1 - gap) * BS
            tile = tiles[at : at + BS, :]
            piece_out[step, :, SPAN - 1 + gap] = tile.reshape(group, strip, BS)
            if gap > 0:
                piece_out[step, :, SPAN - 1 - gap] = tile.T.reshape(group, strip, BS)
        piece_in[step, place] = piece_out[step, place]

        def one(off, inner):
            piece_to(step, off).start()
            return inner

        lax.fori_loop(1, group, one, 0)

    def tail_to(turn_step, gap, turn):
        to = lax.rem(domain + turn, domains)
        return pltpu.make_async_remote_copy(
            src_ref=tail_out.at[turn_step, to, span_of(gap)],
            dst_ref=tail_in.at[turn_step, domain, span_of(gap)],
            send_sem=tail_send.at[turn_step, min(gap, 1)],
            recv_sem=tail_recv.at[turn_step, gap],
            device_id={"aux": to, "blk": mirror(1 - turn_step + gap, side)},
            device_id_type=MESH,
        )

    def tail_sends():
        for turn_step in range(2):
            for gap in range(SPAN):
                for turn in range(domains):
                    if turn > 0 or turn_step == 0 or gap > 0:
                        yield turn_step, gap, turn

    def direct(turn_step, tiles):
        for gap in range(SPAN):
            at = (SPAN - 1 - gap) * BS
            tile = tiles[at : at + BS, :]
            low = (domains, BS // domains, BS)
            tail_out[turn_step, :, SPAN - 1 + gap] = tile.reshape(low).astype(jnp.bfloat16)
            if gap > 0:
                tail_out[turn_step, :, SPAN - 1 - gap] = tile.T.reshape(low).astype(jnp.bfloat16)
        for which, gap, turn in tail_sends():
            if which == turn_step:
                tail_to(turn_step, gap, turn).start()
        if turn_step == 1:
            tail_in[1, domain, :SPAN] = tail_out[1, domain, :SPAN]

    def step(index, carry):
        late = is_tail & (index >= last - 1)

        @pl.when((index > 0) & jnp.logical_not(is_tail & (index == last)))
        def _():
            gather(index - 1)

        @pl.when(late)
        def _():
            gather(index)

        @pl.when(is_tail & (index == last))
        def _():
            ship()

        collect(index)
        tiles = multiply(index)

        @pl.when(jnp.logical_not(late))
        def _():
            pieces(index, tiles)

        for turn_step in range(2):

            @pl.when(is_tail & (index == last - 1 + turn_step))
            def _():
                direct(turn_step, tiles)

        return carry

    lax.fori_loop(0, blocks, step, 0)

    @pl.when(jnp.logical_not(is_tail))
    def _():
        gather(last)
        ship()

    def settle(index, carry):
        settled(slab.at[index, pl.ds(0, depth - rows)], send_sem.at[index])

        @pl.when(jnp.logical_not(is_tail & (index >= last - 1)))
        def _():
            settled(piece_out.at[index, pl.ds(0, group - 1)], piece_send.at[index])

        return carry

    lax.fori_loop(0, blocks, settle, 0)
    settled(sum_out.at[pl.ds(0, half)], cross_send.at[0])
    for gap in range(SPAN):
        for whole in (0, 1):

            @pl.when((rank < gap) if whole else (rank >= gap))
            def _():
                count = half - gap - 1 + whole
                settled(sum_in.at[pl.ds(0, count), span_of(gap)], sum_send.at[gap])


    for gap in range(SPAN):

        @pl.when(rank >= gap)
        def _():
            settled(sum_in.at[pl.ds(0, peers - 1), span_of(gap)], sum_recv.at[gap])

        @pl.when(rank < gap)
        def _():
            settled(sum_in.at[pl.ds(0, half), span_of(gap)], sum_recv.at[gap])

    for turn_step in range(2):
        for gap in range(SPAN):
            wanted = rank == 1 - turn_step + gap
            here = turn_step == 1 and gap == 0

            @pl.when(wanted)
            def _():
                count = domains - 1 if here else domains
                settled(
                    tail_in.at[turn_step, pl.ds(0, count), span_of(gap)],
                    tail_recv.at[turn_step, gap],
                )

    for slot in range(slots):
        where = SPAN - 1 + sign * (slot - (SPAN - 1))
        columns = pl.ds(pl.multiple_of(where * BS, BS), BS)
        for core in range(PAIR):
            total = jnp.zeros((strip, BS), jnp.float32)
            for turn in range(half // PAIR):
                total = total + sum_in[(1 - side) * half + turn * PAIR + core, slots - 1 - slot]
                total = total + sum_in[side * half + turn * PAIR + core, slot]
            out_ref[0, core * strip : (core + 1) * strip, columns] = total * weights[slot]

    for turn_step in range(2):
        for gap in range(SPAN):

            @pl.when(rank == 1 - turn_step + gap)
            def _():
                for slot in range(SPAN) if gap == 0 else [SPAN - 1 + gap]:
                    where = SPAN - 1 + sign * (slot - (SPAN - 1))
                    columns = pl.ds(pl.multiple_of(where * BS, BS), BS)
                    total = tail_in[turn_step, 0, slot].astype(jnp.float32)
                    for sender in range(1, domains):
                        total = total + tail_in[turn_step, sender, slot].astype(jnp.float32)
                    out_ref[0, :, columns] = out_ref[0, :, columns] + total * weights[slot]

    @pl.when(is_tail)
    def _():
        for turn_step in range(2):
            count = domains - turn_step
            settled(tail_out.at[turn_step, pl.ds(0, count), span_of(0)], tail_send.at[turn_step, 0])
            settled(tail_out.at[turn_step, :, pl.ds(SPAN, SPAN - 1)], tail_send.at[turn_step, 1])


def in_hbm(operand):
    return pltpu.with_memory_space_constraint(operand, pltpu.MemorySpace.HBM)


def by_orbital(integrals, metric, pair_list, aux_mask):
    peers = lax.axis_size("blk")
    domains = lax.axis_size("aux")
    depth = metric.shape[1]
    blocks = aux_mask.shape[1]
    group = domains * PAIR
    slots = 2 * SPAN - 1
    strip = BS // group
    return pl.pallas_call(
        functools.partial(tile_kernel, peers, domains, blocks, depth),
        out_shape=jax.ShapeDtypeStruct((1, BS // domains, slots * BS), jnp.float32),
        in_specs=[
            pl.BlockSpec(memory_space=pl.ANY),
            pl.BlockSpec(memory_space=pl.ANY),
            pl.BlockSpec(memory_space=pl.ANY),
            pl.BlockSpec(memory_space=pl.ANY),
        ],
        out_specs=pl.BlockSpec(memory_space=pltpu.VMEM),
        scratch_shapes=[
            pltpu.SMEM(aux_mask.shape, jnp.int32),
            pltpu.SMEM(pair_list.shape[::-1], jnp.int32),
            pltpu.VMEM(metric.shape, jnp.bfloat16),
            pltpu.VMEM((blocks, depth, SUB, BS), jnp.bfloat16),
            pltpu.VMEM((depth // peers * SUB, BS), jnp.float32),
            pltpu.VMEM((depth, SUB * BS), jnp.bfloat16),
            pltpu.VMEM((SUB * depth, BS), jnp.bfloat16),
            pltpu.VMEM(((blocks + SPAN - 1) * BS, SUB * depth), jnp.bfloat16),
            pltpu.VMEM((blocks, group, slots, strip, BS), jnp.float32),
            pltpu.VMEM((blocks, group, slots, strip, BS), jnp.float32),
            pltpu.VMEM((blocks, slots, strip, BS), jnp.float32),
            pltpu.VMEM((peers, slots, strip, BS), jnp.float32),
            pltpu.VMEM((2, domains, slots, BS // domains, BS), jnp.bfloat16),
            pltpu.VMEM((2, domains, slots, BS // domains, BS), jnp.bfloat16),
            pltpu.SMEM((slots,), jnp.float32),
            pltpu.SemaphoreType.DMA((blocks,)),
            pltpu.SemaphoreType.DMA((blocks,)),
            pltpu.SemaphoreType.DMA((blocks,)),
            pltpu.SemaphoreType.DMA((blocks,)),
            pltpu.SemaphoreType.DMA((SPAN,)),
            pltpu.SemaphoreType.DMA((SPAN,)),
            pltpu.SemaphoreType.DMA((1,)),
            pltpu.SemaphoreType.DMA((2, 2)),
            pltpu.SemaphoreType.DMA((2, SPAN)),
            pltpu.SemaphoreType.DMA((3,)),
        ],
        compiler_params=pltpu.CompilerParams(
            collective_id=0, has_side_effects=True, vmem_limit_bytes=36 * 1024 * 1024
        ),
    )(*[in_hbm(operand) for operand in (aux_mask, pair_list.T, metric, integrals)])


def from_behind(array, axis, by):
    peers = lax.axis_size(axis)
    pairs = [(i, i + by) for i in range(peers) if 0 <= i + by < peers]
    return lax.ppermute(array, axis, pairs)


def fit_block(metric, slab_piece, mask_rows):
    fitted = jnp.einsum("pq,qjn->pjn", metric, slab_piece, preferred_element_type=jnp.float32)
    return (fitted * mask_rows[:, None, None]).astype(jnp.bfloat16)


def by_block(integrals, metric, pair_list, aux_mask):
    block_count = aux_mask.shape[1]
    position = lax.axis_index("blk")
    block_ids = jnp.arange(block_count, dtype=jnp.int32)
    offsets = jnp.arange(SPAN, dtype=jnp.int32)
    col_gap = pair_list[:, 1] - pair_list[:, 0]
    hits = (pair_list[:, 0][:, None] == position) & (col_gap[:, None] == offsets[None, :])
    listed = jnp.sum(hits.astype(jnp.int32), axis=0)
    one_hot = (block_ids == position).astype(jnp.int32)
    column = jnp.sum(aux_mask * one_hot[None, :], axis=1)
    own_mask = jnp.repeat(column, QB).astype(jnp.float32)
    own_block = fit_block(
        metric, lax.all_to_all(integrals, "blk", split_axis=2, concat_axis=0, tiled=True), own_mask
    )
    partners = [own_block]
    current = own_block
    for turn_index in range(SPAN - 1):
        current = from_behind(current, "blk", -1)
        partners.append(current)
    flat_own = partners[0].reshape(-1, BS)

    def make_tile(partner):
        return lax.dot_general(
            flat_own,
            partner.reshape(-1, BS),
            (((0,), (0,)), ((), ())),
            preferred_element_type=jnp.float32,
        )

    tile_list = [
        make_tile(partners[offset]) * listed[offset].astype(jnp.float32) for offset in range(SPAN)
    ]
    upper_tiles = jnp.stack(tile_list)
    mirror_tiles = jnp.stack([jnp.transpose(tile_list[offset]) for offset in range(1, SPAN)])
    lower_tiles = []
    moving = mirror_tiles
    for turn_index in range(SPAN - 1):
        moving = from_behind(moving.astype(jnp.bfloat16), "blk", 1).astype(moving.dtype)
        lower_tiles.append(moving[0])
        moving = moving[1:]
    whole_band = jnp.concatenate(
        [jnp.stack([lower_tiles[SPAN - 2 - slot] for slot in range(SPAN - 1)]), upper_tiles], axis=0
    )
    band_parts = lax.psum_scatter(whole_band, "aux", scatter_dimension=1, tiled=True)
    pieces = [band_parts[slot] for slot in range(2 * SPAN - 1)]
    band_rows = jnp.concatenate(pieces, axis=1)
    return band_rows[None]


def local(integrals, metric, pair_list, aux_mask):
    peers = lax.axis_size("blk")
    blocks = aux_mask.shape[1]
    strips = BS % (8 * PAIR * lax.axis_size("aux")) == 0 and peers == 4 * PAIR
    whole_tiles = integrals.shape[1] == SUB * peers and blocks == peers and strips
    if whole_tiles:
        return by_orbital(integrals, metric, pair_list, aux_mask)
    return by_block(integrals, metric, pair_list, aux_mask)


def solution(mesh):
    return jax.shard_map(
        local,
        mesh=mesh,
        in_specs=(P(("aux", "blk"), None, None), P("aux", None), P(), P("aux", None)),
        out_specs=P("blk", "aux", None),
        check_vma=False,
    )
```
